32 devices in a mesh: dp: 4 (over z), vocab: 8 (over y, x, core).
Axes of the slice: x: 2, y: 2, z: 4, core: 2. Of those that a mesh axis runs over, the one named last changes fastest.
Arguments:
- token_ids: int32 [8192], P(('dp', 'vocab')), may hold values from 0 to 152063, as said below
- token_count: int32 [32], P(('dp', 'vocab')), may hold values from 16 to 256
- out_grads: bfloat16 [8192, 5120], P(('dp', 'vocab')), may hold values from -18 to 18
- master_rows: float32 [4096, 5120], P('vocab', 'dp'), may hold values from -0.8 to 0.8
- first_moment: float32 [4096, 5120], P('vocab', 'dp'), may hold values from -4 to 4
- second_moment: float32 [4096, 5120], P('vocab', 'dp'), may hold values from 0.001 to 1
Outputs:
- new_master: float32 [4096, 5120], P('vocab', 'dp')
- new_first: float32 [4096, 5120], P('vocab', 'dp')
- new_second: float32 [4096, 5120], P('vocab', 'dp')
- table_rows: bfloat16 [4096, 5120], P('vocab')
The draws below stay inside these ranges and needn't reach their ends.
Inputs may be any that keep to these rules, and one draw needn't show every extreme that they name: `token_ids`: within each block of 256 slots, among the live slots (the first token_count of the block) at most 8 have ids in the new rows j * 512 + 147968 to (j + 1) * 512 + 147967 for any one j, and for some j exactly 8 in every block. Slots past token_count hold ids of new rows that are to be ignored.
All inputs are finite; a program needn't handle non-finite values.
Results may differ from the reference program's by a relative error of at most 0.001.
Values may be sent and summed in bfloat16 or wider, within the bound.
A program may use at most 64 MiB of HBM per device.

```python
import math
import jax
import jax.numpy as jnp
from jax import lax

D = 5120
VOCAB = 152064
T_DEV = 256
NEW_DEV = 512
CAP = 8
NEW = 4096
TOKENS = 8192


def layout_tokens(key):
    key = jax.random.fold_in(key, 7)
    owners = NEW // NEW_DEV
    blocks = TOKENS // T_DEV
    keys = jax.random.split(key, 7)
    hottest = jax.random.randint(keys[0], (2,), 0, owners)
    baseline = jax.random.randint(keys[1], (blocks, owners), 0, CAP + 1)
    owner_axis = jnp.arange(owners)
    is_hot = (owner_axis[None, :] == hottest[0]) | (owner_axis[None, :] == hottest[1])
    per_owner = jnp.where(is_hot, CAP, baseline)
    ends = jnp.cumsum(per_owner, axis=1)
    new_total = ends[:, -1]
    extra = jax.random.randint(keys[2], (blocks,), 0, 1 << 20)
    live_count = new_total + extra % (T_DEV - new_total + 1)
    slots = jnp.arange(T_DEV)
    owner_of = jnp.sum((slots[None, :, None] >= ends[:, None, :]).astype(jnp.int32), axis=2)
    owner_of = jnp.minimum(owner_of, owners - 1)
    is_new = slots[None, :] < new_total[:, None]
    row_pick = jax.random.randint(keys[3], (blocks, T_DEV), 0, NEW_DEV)
    new_ids = VOCAB - NEW + owner_of * NEW_DEV + row_pick
    old_ids = jax.random.randint(keys[4], (blocks, T_DEV), 0, VOCAB - NEW)
    pad_ids = jax.random.randint(keys[5], (blocks, T_DEV), VOCAB - NEW, VOCAB)
    ordered = jnp.where(is_new, new_ids, old_ids)
    scores = jax.random.randint(keys[6], (blocks, T_DEV), 0, 1 << 20)
    is_head = slots[None, :] < live_count[:, None]
    keyed = jnp.where(is_head, scores * T_DEV + slots[None, :], (1 << 20) * T_DEV + slots[None, :])
    order = jnp.argsort(keyed, axis=1)
    shuffled = jnp.take_along_axis(ordered, order, axis=1)
    final_ids = jnp.where(is_head, shuffled, pad_ids)
    return (final_ids.reshape(TOKENS).astype(jnp.int32), live_count.astype(jnp.int32))


def draw_token_ids(key, part):
    return layout_tokens(key)[0]


def draw_token_count(key, part):
    return layout_tokens(key)[1]


def levels(stream_key, extent, pieces, smallest, largest):
    gain, own = 1.0, jax.random.fold_in(stream_key, 6)
    for axis_at, shards_of in pieces:
        steps = jnp.exp(jax.random.uniform(jax.random.fold_in(own, axis_at), (shards_of,), jnp.float32, smallest / len(pieces), largest / len(pieces)))
        gain = gain * jnp.repeat(steps, extent[axis_at] // shards_of).reshape([-1 if axis == axis_at else 1 for axis in range(len(extent))])
    return gain


def centred(stream_key, shape, width, most, pieces=(), held_as=jnp.bfloat16):
    level = levels(stream_key, shape, pieces, -0.22, 0.18) if pieces else 1.0
    entries = jax.random.normal(stream_key, shape, jnp.float32) * width * level
    return jnp.minimum(jnp.maximum(entries, -most), most).astype(held_as)


def setup_inputs(seed: int = 0) -> dict:
    seeds = jax.random.split(jax.random.key(seed), 7)
    return {
        "token_ids": draw_token_ids(jax.random.fold_in(seeds[6], 71), 0),
        "token_count": draw_token_count(jax.random.fold_in(seeds[6], 71), 0),
        "out_grads": centred(seeds[2], (TOKENS, D), 3.0, 18.0, ((0, 32),)),
        "master_rows": centred(seeds[3], (NEW, D), 0.2, 0.8, ((0, 8), (1, 4)), jnp.float32),
        "first_moment": centred(seeds[4], (NEW, D), 0.5, 4.0, ((0, 8), (1, 4)), jnp.float32),
        "second_moment": jnp.clip(jnp.exp(math.log(1.0) - 6.9077552 * jax.random.uniform(seeds[5], (NEW, D), jnp.float32) ** levels(seeds[5], (NEW, D), ((0, 8), (1, 4)), -0.2, 0.2)), 0.001, 1.0),
    }


beta_one = 0.9
beta_two = 0.999
corr_one = 1.0 - 0.9 ** 10
corr_two = 1.0 - 0.999 ** 10
learn_rate = 0.01
epsilon = 1e-08

def reference(token_ids, token_count, out_grads, master_rows, first_moment, second_moment):
    first_new = VOCAB - NEW
    blocks = token_ids.shape[0] // T_DEV
    ids_blocks = token_ids.reshape(blocks, T_DEV)
    position = jnp.arange(T_DEV)
    is_live = (position[None, :] < token_count[:, None]) & (ids_blocks >= first_new)
    segment = jnp.where(is_live, ids_blocks - first_new, NEW)
    grad_blocks = out_grads.reshape(blocks, T_DEV, D)

    def add_block(running, inputs):
        ids_block, grad_block = inputs
        summed = jax.ops.segment_sum(grad_block.astype(jnp.float32), ids_block, num_segments=NEW + 1)
        return (running + summed, None)
    grad_all, _ = lax.scan(add_block, jnp.zeros((NEW + 1, D), jnp.float32), (segment, grad_blocks))
    gradient = grad_all[:NEW]
    new_first = beta_one * first_moment + (1.0 - beta_one) * gradient
    new_second = beta_two * second_moment + (1.0 - beta_two) * gradient * gradient
    update = new_first / corr_one / (jnp.sqrt(new_second / corr_two) + epsilon)
    new_master = master_rows - learn_rate * update
    return (new_master, new_first, new_second, new_master.astype(jnp.bfloat16))
```

```python
import functools

import jax
import jax.numpy as jnp
from jax import lax
from jax.experimental import pallas as pl
from jax.experimental.pallas import tpu as pltpu
from jax.sharding import PartitionSpec as P

VOCAB = 152064
CAP = 8
LANES = 128
CHUNKS = 8
MESH = pl.DeviceIdType.MESH


beta_one = 0.9
beta_two = 0.999
corr_one = 1.0 - 0.9**10
corr_two = 1.0 - 0.999**10
learn_rate = 0.01
epsilon = 1e-08


def exchange_kernel(groups, owners, out_ref, arr_ref, send_sem, recv_sem, own_sem):
    my_dp, my_vocab = lax.axis_index("dp"), lax.axis_index("vocab")
    total = groups * owners
    me = my_dp * owners + my_vocab
    barrier = pltpu.get_barrier_semaphore()

    def target(k):
        other = lax.rem(me + k, total)
        return other // owners, lax.rem(other, owners)

    def greet(k, carry):
        pl.semaphore_signal(barrier, inc=1, device_id=target(k), device_id_type=MESH)
        return carry

    lax.fori_loop(1, total, greet, 0)
    pl.semaphore_wait(barrier, total - 1)

    own = pltpu.make_async_copy(out_ref.at[my_dp, my_vocab], arr_ref.at[me], own_sem)
    own.start()

    def copy(k):
        to_dp, to_vocab = target(k)
        return pltpu.make_async_remote_copy(
            src_ref=out_ref.at[to_dp, to_vocab],
            dst_ref=arr_ref.at[me],
            send_sem=send_sem.at[k],
            recv_sem=recv_sem.at[k],
            device_id=(to_dp, to_vocab),
            device_id_type=MESH,
        )

    def send(k, carry):
        copy(k).start()
        return carry

    lax.fori_loop(1, total, send, 0)

    def finish(k, carry):
        copy(k).wait_send()
        sender = lax.rem(me - k + total, total)
        pltpu.make_async_remote_copy(
            src_ref=out_ref.at[my_dp, my_vocab],
            dst_ref=arr_ref.at[sender],
            send_sem=send_sem.at[k],
            recv_sem=recv_sem.at[k],
            device_id=target(k),
            device_id_type=MESH,
        ).wait_recv()
        return carry

    lax.fori_loop(1, total, finish, 0)
    own.wait()


def exchange(outgoing):
    groups, owners, cap, width = outgoing.shape
    total = groups * owners
    return pl.pallas_call(
        functools.partial(exchange_kernel, groups, owners),
        out_shape=jax.ShapeDtypeStruct((total, cap, width), outgoing.dtype),
        in_specs=[pl.BlockSpec(memory_space=pltpu.VMEM)],
        out_specs=pl.BlockSpec(memory_space=pltpu.VMEM),
        scratch_shapes=[
            pltpu.SemaphoreType.DMA((total,)),
            pltpu.SemaphoreType.DMA((total,)),
            pltpu.SemaphoreType.DMA,
        ],
        compiler_params=pltpu.CompilerParams(collective_id=0, has_side_effects=True),
        name="exchange",
    )(outgoing)


def gather_kernel(groups, block_ref, table_ref, left_sem, right_sem, recv_sem, own_sem):
    my_dp = lax.axis_index("dp")
    rows, columns = block_ref.shape
    step_rows = rows // CHUNKS
    barrier = pltpu.get_barrier_semaphore()
    has_left, has_right = my_dp > 0, my_dp < groups - 1

    @pl.when(has_left)
    def _():
        pl.semaphore_signal(barrier, inc=1, device_id={"dp": my_dp - 1}, device_id_type=MESH)

    @pl.when(has_right)
    def _():
        pl.semaphore_signal(barrier, inc=1, device_id={"dp": my_dp + 1}, device_id_type=MESH)

    pl.semaphore_wait(barrier, has_left.astype(jnp.int32) + has_right.astype(jnp.int32))

    def place(block, chunk):
        start = pl.multiple_of(block * columns, LANES)
        return table_ref.at[pl.ds(chunk * step_rows, step_rows), pl.ds(start, columns)]

    own = pltpu.make_async_copy(
        block_ref, table_ref.at[:, pl.ds(pl.multiple_of(my_dp * columns, LANES), columns)], own_sem
    )
    own.start()

    def copy(block, chunk, step, sem, to_dp):
        source = (
            block_ref.at[pl.ds(chunk * step_rows, step_rows), :] if step == 0 else place(block, chunk)
        )
        return pltpu.make_async_remote_copy(
            src_ref=source,
            dst_ref=place(block, chunk),
            send_sem=sem.at[step, chunk],
            recv_sem=recv_sem.at[block, chunk],
            device_id={"dp": to_dp},
            device_id_type=MESH,
        )

    def each(act):
        for step in range(groups):
            for chunk in range(CHUNKS):
                upper, lower = my_dp + step, my_dp - step
                pl.when(upper < groups)(functools.partial(act, upper, chunk, step, left_sem, my_dp - 1, has_left))
                pl.when(lower >= 0)(functools.partial(act, lower, chunk, step, right_sem, my_dp + 1, has_right))

    def start(block, chunk, step, sem, to_dp, sends):
        if step > 0:
            copy(block, chunk, step, sem, my_dp).wait_recv()

        @pl.when(sends)
        def _():
            copy(block, chunk, step, sem, to_dp).start()

    def drain(block, chunk, step, sem, to_dp, sends):
        @pl.when(sends)
        def _():
            copy(block, chunk, step, sem, to_dp).wait_send()

    each(start)
    each(drain)
    own.wait()


def gather(block, groups):
    rows, columns = block.shape
    return pl.pallas_call(
        functools.partial(gather_kernel, groups),
        out_shape=jax.ShapeDtypeStruct((rows, columns * groups), block.dtype),
        in_specs=[pl.BlockSpec(memory_space=pl.ANY)],
        out_specs=pl.BlockSpec(memory_space=pl.ANY),
        scratch_shapes=[
            pltpu.SemaphoreType.DMA((groups, CHUNKS)),
            pltpu.SemaphoreType.DMA((groups, CHUNKS)),
            pltpu.SemaphoreType.DMA((groups, CHUNKS)),
            pltpu.SemaphoreType.DMA,
        ],
        compiler_params=pltpu.CompilerParams(collective_id=1, has_side_effects=True),
        name="gather",
    )(block)


def body(token_ids, token_count, out_grads, master_rows, first_moment, second_moment):
    owners = lax.axis_size("vocab")
    groups = lax.axis_size("dp")
    rows_own, columns = master_rows.shape
    tok_slots = token_ids.shape[0]
    first_new = VOCAB - rows_own * owners
    position = jnp.arange(tok_slots)
    is_live = (position < token_count[0]) & (token_ids >= first_new)
    new_index = token_ids - first_new
    owner_of = jnp.where(is_live, new_index // rows_own, -1)
    row_in_owner = new_index % rows_own
    earlier = (owner_of[:, None] == owner_of[None, :]) & (position[:, None] < position[None, :])
    my_rank = jnp.sum(earlier.astype(jnp.int32), axis=0)
    slot_index = jnp.where(is_live, owner_of * CAP + my_rank, -1)
    placing = jnp.arange(owners * CAP)[:, None] == slot_index[None, :]
    outgoing = jnp.dot(
        placing.astype(jnp.bfloat16), out_grads, preferred_element_type=jnp.float32
    ).astype(jnp.bfloat16)
    slot_row = jnp.max(jnp.where(placing, row_in_owner[None, :], -1), axis=1)
    upper_part = jnp.where(slot_row >= 0, slot_row // 16, -1)
    lower_part = jnp.where(slot_row >= 0, slot_row % 16, 0)
    lane = jnp.arange(LANES)[None, :]
    row_pairs = jnp.where(lane == 0, upper_part[:, None], jnp.where(lane == 1, lower_part[:, None], 0))
    row_pairs = row_pairs.astype(jnp.bfloat16).reshape(1, owners, CAP, LANES)
    outgoing = outgoing.reshape(owners, CAP, groups, columns).transpose(2, 0, 1, 3)
    outgoing = jnp.concatenate(
        [outgoing, jnp.broadcast_to(row_pairs, (groups, owners, CAP, LANES))], axis=3
    )
    arrived = exchange(outgoing).reshape(-1, columns + LANES)
    pairs = arrived[:, columns : columns + 2].astype(jnp.float32)
    decoded = pairs[:, 0] * 16.0 + pairs[:, 1]
    selector = decoded[None, :] == jnp.arange(rows_own, dtype=jnp.float32)[:, None]
    gradient = jnp.dot(
        selector.astype(jnp.bfloat16), arrived[:, :columns], preferred_element_type=jnp.float32
    )
    new_first = beta_one * first_moment + (1.0 - beta_one) * gradient
    new_second = beta_two * second_moment + (1.0 - beta_two) * gradient * gradient
    update = new_first / corr_one / (jnp.sqrt(new_second / corr_two) + epsilon)
    new_master = master_rows - learn_rate * update
    table_rows = gather(new_master.astype(jnp.bfloat16), groups)
    return (new_master, new_first, new_second, table_rows)


def solution(mesh):
    return jax.shard_map(
        body,
        mesh=mesh,
        in_specs=(
            P(("dp", "vocab")),
            P(("dp", "vocab")),
            P(("dp", "vocab"), None),
            P("vocab", "dp"),
            P("vocab", "dp"),
            P("vocab", "dp"),
        ),
        out_specs=(P("vocab", "dp"), P("vocab", "dp"), P("vocab", "dp"), P("vocab", None)),
        check_vma=False,
    )
```

```python
import functools

import jax
import jax.numpy as jnp
from jax import lax
from jax.experimental import pallas as pl
from jax.experimental.pallas import tpu as pltpu
from jax.sharding import PartitionSpec as P

VOCAB = 152064
CAP = 8
LANES = 128
CHUNKS = 8
KEPT = 4
MESH = pl.DeviceIdType.MESH


beta_one = 0.9
beta_two = 0.999
corr_one = 1.0 - 0.9**10
corr_two = 1.0 - 0.999**10
learn_rate = 0.01
epsilon = 1e-08


def adam(gradient, master, first, second):
    new_first = beta_one * first + (1.0 - beta_one) * gradient
    new_second = beta_two * second + (1.0 - beta_two) * gradient * gradient
    update = new_first / corr_one / (jnp.sqrt(new_second / corr_two) + epsilon)
    return master - learn_rate * update, new_first, new_second


def step_kernel(
    groups,
    owners,
    kept,
    out_ref,
    master_hbm,
    first_hbm,
    second_hbm,
    table_ref,
    arr_ref,
    master_ref,
    first_ref,
    second_ref,
    block_ref,
    send_sem,
    arrive_sem,
    left_sem,
    right_sem,
    recv_sem,
    own_sem,
    load_sem,
):
    my_dp, my_vocab = lax.axis_index("dp"), lax.axis_index("vocab")
    total = groups * owners
    me = my_dp * owners + my_vocab
    rows, columns = master_ref.shape
    step_rows = rows // CHUNKS
    barrier = pltpu.get_barrier_semaphore()
    has_left, has_right = my_dp > 0, my_dp < groups - 1

    loads = [
        pltpu.make_async_copy(src, dst, load_sem.at[i])
        for i, (src, dst) in enumerate(
            ((master_hbm, master_ref), (first_hbm, first_ref), (second_hbm, second_ref))
        )
    ]
    for load in loads:
        load.start()

    def greet(k, carry):
        other = lax.rem(me + k, total)
        pl.semaphore_signal(
            barrier, inc=1, device_id=(other // owners, lax.rem(other, owners)), device_id_type=MESH
        )
        return carry

    lax.fori_loop(1, total, greet, 0)
    own = pltpu.make_async_copy(out_ref.at[my_dp, my_vocab], arr_ref.at[me], own_sem.at[0])
    own.start()
    pl.semaphore_wait(barrier, total - 1)

    def send_copy(k):
        to_dp = lax.rem(k // owners + 1, groups)
        to_vocab = lax.rem(my_vocab + lax.rem(k, owners), owners)
        here = (to_dp == my_dp) & (to_vocab == my_vocab)
        return here, pltpu.make_async_remote_copy(
            src_ref=out_ref.at[to_dp, to_vocab],
            dst_ref=arr_ref.at[me],
            send_sem=send_sem.at[k],
            recv_sem=arrive_sem.at[me],
            device_id=(to_dp, to_vocab),
            device_id_type=MESH,
        )

    def send(k, carry):
        here, copy = send_copy(k)

        @pl.when(jnp.logical_not(here))
        def _():
            copy.start()

        return carry

    lax.fori_loop(0, total, send, 0)

    def arrive(k, carry):
        sender = lax.rem(me + k, total)
        pltpu.make_async_remote_copy(
            src_ref=out_ref.at[my_dp, my_vocab],
            dst_ref=arr_ref.at[sender],
            send_sem=send_sem.at[k],
            recv_sem=arrive_sem.at[sender],
            device_id=(sender // owners, lax.rem(sender, owners)),
            device_id_type=MESH,
        ).wait_recv()
        return carry

    for load in loads:
        load.wait()
    own.wait()
    lax.fori_loop(1, total, arrive, 0)

    tokens = total * arr_ref.shape[1]
    pairs = arr_ref[:, :, columns:].astype(jnp.float32).reshape(tokens, LANES)
    decoded = jnp.broadcast_to(pairs[:, 0:1] * 16.0 + pairs[:, 1:2], (tokens, LANES)).T[0:1, :]
    grads = arr_ref[:, :, :columns].astype(jnp.float32).reshape(tokens, columns).astype(jnp.bfloat16)

    def place(block, chunk):
        start = pl.multiple_of(block * columns, LANES)
        return table_ref.at[pl.ds(chunk * step_rows, step_rows), pl.ds(start, columns)]

    def copy(block, chunk, step, sem, to_dp):
        source = (
            block_ref.at[pl.ds(chunk * step_rows, step_rows), :] if step == 0 else place(block, chunk)
        )
        return pltpu.make_async_remote_copy(
            src_ref=source,
            dst_ref=place(block, chunk),
            send_sem=sem.at[step, chunk],
            recv_sem=recv_sem.at[block, chunk],
            device_id={"dp": to_dp},
            device_id_type=MESH,
        )

    def both(act, step, chunk):
        upper, lower = my_dp + step, my_dp - step
        pl.when(upper < groups)(functools.partial(act, upper, chunk, step, left_sem, my_dp - 1, has_left))
        pl.when(lower >= 0)(functools.partial(act, lower, chunk, step, right_sem, my_dp + 1, has_right))

    def held_back(step, chunk):
        return step >= groups - 1 and chunk >= kept

    def start(block, chunk, step, sem, to_dp, sends):
        if step > 0:
            copy(block, chunk, step, sem, my_dp).wait_recv()
        if not held_back(step + 1, chunk):

            @pl.when(sends)
            def _():
                copy(block, chunk, step, sem, to_dp).start()

    def drain(block, chunk, step, sem, to_dp, sends):
        if not held_back(step + 1, chunk):

            @pl.when(sends)
            def _():
                copy(block, chunk, step, sem, to_dp).wait_send()

    row_iota = lax.broadcasted_iota(jnp.int32, (step_rows, tokens), 0)
    for chunk in range(CHUNKS):
        here = pl.ds(chunk * step_rows, step_rows)
        selector = decoded == (row_iota + chunk * step_rows).astype(jnp.float32)
        gradient = jnp.dot(
            selector.astype(jnp.float32).astype(jnp.bfloat16), grads, preferred_element_type=jnp.float32
        )
        master = adam(gradient, master_ref[here, :], first_ref[here, :], second_ref[here, :])[0]
        block_ref[here, :] = master.astype(jnp.bfloat16)
        if chunk > 0:
            both(start, 0, chunk - 1)
    both(start, 0, CHUNKS - 1)
    own_block = pltpu.make_async_copy(
        block_ref,
        table_ref.at[:, pl.ds(pl.multiple_of(my_dp * columns, LANES), columns)],
        own_sem.at[1],
    )
    own_block.start()
    for step in range(1, groups):
        for chunk in range(CHUNKS):
            if not held_back(step, chunk):
                both(start, step, chunk)
    for step in range(groups):
        for chunk in range(CHUNKS):
            if not held_back(step, chunk):
                both(drain, step, chunk)

    def sent(k, carry):
        here, copy = send_copy(k)

        @pl.when(jnp.logical_not(here))
        def _():
            copy.wait_send()

        return carry

    lax.fori_loop(0, total, sent, 0)
    own_block.wait()


def exchange_and_gather(outgoing, master, first, second, kept):
    groups, owners, cap, width = outgoing.shape
    total = groups * owners
    rows, columns = master.shape
    return pl.pallas_call(
        functools.partial(step_kernel, groups, owners, kept),
        out_shape=(
            jax.ShapeDtypeStruct((rows, columns * groups), jnp.bfloat16),
            jax.ShapeDtypeStruct((total, cap, width), outgoing.dtype),
        ),
        in_specs=[pl.BlockSpec(memory_space=pltpu.VMEM)] + [pl.BlockSpec(memory_space=pl.ANY)] * 3,
        out_specs=(pl.BlockSpec(memory_space=pl.ANY), pl.BlockSpec(memory_space=pltpu.VMEM)),
        scratch_shapes=[
            pltpu.VMEM((rows, columns), jnp.float32),
            pltpu.VMEM((rows, columns), jnp.float32),
            pltpu.VMEM((rows, columns), jnp.float32),
            pltpu.VMEM((rows, columns), jnp.bfloat16),
            pltpu.SemaphoreType.DMA((total,)),
            pltpu.SemaphoreType.DMA((total,)),
            pltpu.SemaphoreType.DMA((groups, CHUNKS)),
            pltpu.SemaphoreType.DMA((groups, CHUNKS)),
            pltpu.SemaphoreType.DMA((groups, CHUNKS)),
            pltpu.SemaphoreType.DMA((2,)),
            pltpu.SemaphoreType.DMA((3,)),
        ],
        compiler_params=pltpu.CompilerParams(collective_id=0, has_side_effects=True),
        name="exchange_and_gather",
    )(outgoing, master, first, second)


def copy_kernel(src_ref, dst_ref):
    dst_ref[...] = src_ref[...]


def fresh_copy(table):
    rows, width = table.shape
    block = pl.BlockSpec((rows // CHUNKS, width), lambda i: (i, 0))
    return pl.pallas_call(
        copy_kernel,
        out_shape=jax.ShapeDtypeStruct(table.shape, table.dtype),
        grid=(CHUNKS,),
        in_specs=[block],
        out_specs=block,
        cost_estimate=pl.CostEstimate(flops=0, bytes_accessed=4 * rows * width, transcendentals=0),
        name="fresh_copy",
    )(table)


def patch_kernel(groups, tail_ref, old_ref, table_ref, sem):
    my_dp = lax.axis_index("dp")
    rows, columns = tail_ref.shape
    top = table_ref.shape[0] - rows
    far = pl.multiple_of(jnp.where(my_dp == 0, groups - 1, 0) * columns, LANES)

    @pl.when((my_dp == 0) | (my_dp == groups - 1))
    def _():
        copy = pltpu.make_async_copy(tail_ref, table_ref.at[pl.ds(top, rows), pl.ds(far, columns)], sem)
        copy.start()
        copy.wait()


def patch(tail, table, groups):
    return pl.pallas_call(
        functools.partial(patch_kernel, groups),
        out_shape=jax.ShapeDtypeStruct(table.shape, table.dtype),
        in_specs=[pl.BlockSpec(memory_space=pltpu.VMEM), pl.BlockSpec(memory_space=pl.ANY)],
        out_specs=pl.BlockSpec(memory_space=pl.ANY),
        scratch_shapes=[pltpu.SemaphoreType.DMA],
        input_output_aliases={1: 0},
        name="patch",
    )(tail, table)


def body(token_ids, token_count, out_grads, master_rows, first_moment, second_moment):
    owners = lax.axis_size("vocab")
    groups = lax.axis_size("dp")
    rows_own, columns = master_rows.shape
    tok_slots = token_ids.shape[0]
    first_new = VOCAB - rows_own * owners
    position = jnp.arange(tok_slots)
    is_live = (position < token_count[0]) & (token_ids >= first_new)
    new_index = token_ids - first_new
    owner_of = jnp.where(is_live, new_index // rows_own, -1)
    row_in_owner = new_index % rows_own
    earlier = (owner_of[:, None] == owner_of[None, :]) & (position[:, None] < position[None, :])
    my_rank = jnp.sum(earlier.astype(jnp.int32), axis=0)
    slot_index = jnp.where(is_live, owner_of * CAP + my_rank, -1)
    placing = jnp.arange(owners * CAP)[:, None] == slot_index[None, :]
    outgoing = jnp.dot(
        placing.astype(jnp.bfloat16), out_grads, preferred_element_type=jnp.float32
    ).astype(jnp.bfloat16)
    slot_row = jnp.max(jnp.where(placing, row_in_owner[None, :], -1), axis=1)
    upper_part = jnp.where(slot_row >= 0, slot_row // 16, -1)
    lower_part = jnp.where(slot_row >= 0, slot_row % 16, 0)
    lane = jnp.arange(LANES)[None, :]
    row_pairs = jnp.where(lane == 0, upper_part[:, None], jnp.where(lane == 1, lower_part[:, None], 0))
    row_pairs = row_pairs.astype(jnp.bfloat16).reshape(1, owners, CAP, LANES)
    outgoing = outgoing.reshape(owners, CAP, groups, columns).transpose(2, 0, 1, 3)
    outgoing = jnp.concatenate(
        [outgoing, jnp.broadcast_to(row_pairs, (groups, owners, CAP, LANES))], axis=3
    )
    kept = KEPT if groups >= 4 else CHUNKS
    table, arrived = exchange_and_gather(outgoing, master_rows, first_moment, second_moment, kept)
    if kept < CHUNKS:
        my_dp = lax.axis_index("dp")
        top = rows_own // CHUNKS * kept
        sent = jnp.where(my_dp == 1, groups - 1, 0) * columns
        tail = lax.dynamic_slice(table, (top, sent), (rows_own - top, columns))
        tail = lax.ppermute(tail, "dp", [(1, 0), (groups - 2, groups - 1)])
        table = fresh_copy(table)
    arrived = arrived.reshape(-1, columns + LANES)
    pairs = arrived[:, columns : columns + 2].astype(jnp.float32)
    decoded = pairs[:, 0] * 16.0 + pairs[:, 1]
    selector = decoded[None, :] == jnp.arange(rows_own, dtype=jnp.float32)[:, None]
    gradient = jnp.dot(
        selector.astype(jnp.bfloat16), arrived[:, :columns], preferred_element_type=jnp.float32
    )
    new_master, new_first, new_second = adam(gradient, master_rows, first_moment, second_moment)
    if kept < CHUNKS:
        table = patch(tail, table, groups)
    return (new_master, new_first, new_second, table)


def solution(mesh):
    return jax.shard_map(
        body,
        mesh=mesh,
        in_specs=(
            P(("dp", "vocab")),
            P(("dp", "vocab")),
            P(("dp", "vocab"), None),
            P("vocab", "dp"),
            P("vocab", "dp"),
            P("vocab", "dp"),
        ),
        out_specs=(P("vocab", "dp"), P("vocab", "dp"), P("vocab", "dp"), P("vocab", None)),
        check_vma=False,
    )
```

```python
import functools

import jax
import jax.numpy as jnp
from jax import lax
from jax.experimental import pallas as pl
from jax.experimental.pallas import tpu as pltpu
from jax.sharding import PartitionSpec as P

VOCAB = 152064
CAP = 8
LANES = 128
CHUNKS = 8
KEPT = 8
MESH = pl.DeviceIdType.MESH


beta_one = 0.9
beta_two = 0.999
corr_one = 1.0 - 0.9**10
corr_two = 1.0 - 0.999**10
learn_rate = 0.01
epsilon = 1e-08


def adam(gradient, master, first, second):
    new_first = beta_one * first + (1.0 - beta_one) * gradient
    new_second = beta_two * second + (1.0 - beta_two) * gradient * gradient
    update = new_first / corr_one / (jnp.sqrt(new_second / corr_two) + epsilon)
    return master - learn_rate * update, new_first, new_second


def step_kernel(
    groups,
    owners,
    kept,
    out_ref,
    ids_ref,
    master_hbm,
    first_hbm,
    second_hbm,
    table_ref,
    master_ref,
    first_ref,
    second_ref,
    arr_ref,
    tag_ref,
    block_ref,
    send_sem,
    arrive_sem,
    tag_send_sem,
    tag_sem,
    left_sem,
    right_sem,
    recv_sem,
    own_sem,
    load_sem,
):
    my_dp, my_vocab = lax.axis_index("dp"), lax.axis_index("vocab")
    total = groups * owners
    me = my_dp * owners + my_vocab
    rows, columns = master_ref.shape
    step_rows = rows // CHUNKS
    barrier = pltpu.get_barrier_semaphore()
    has_left, has_right = my_dp > 0, my_dp < groups - 1

    loads = [
        pltpu.make_async_copy(src, dst, load_sem.at[i])
        for i, (src, dst) in enumerate(
            ((master_hbm, master_ref), (first_hbm, first_ref), (second_hbm, second_ref))
        )
    ]
    for load in loads:
        load.start()

    def greet(k, carry):
        other = lax.rem(me + k, total)
        pl.semaphore_signal(
            barrier, inc=1, device_id=(other // owners, lax.rem(other, owners)), device_id_type=MESH
        )
        return carry

    lax.fori_loop(1, total, greet, 0)
    def part(to_dp, to_vocab):
        row = pl.multiple_of(to_vocab * CAP, CAP)
        return out_ref.at[pl.ds(row, CAP), pl.ds(pl.multiple_of(to_dp * columns, LANES), columns)]

    own = pltpu.make_async_copy(part(my_dp, my_vocab), arr_ref.at[me], own_sem.at[0])
    own.start()
    own_tag = pltpu.make_async_copy(ids_ref.at[my_vocab], tag_ref.at[me], own_sem.at[2])
    own_tag.start()
    pl.semaphore_wait(barrier, total - 1)

    def pair(k, slot, to_dp, to_vocab):
        return (
            pltpu.make_async_remote_copy(
                src_ref=ids_ref.at[to_vocab],
                dst_ref=tag_ref.at[slot],
                send_sem=tag_send_sem.at[k],
                recv_sem=tag_sem.at[slot],
                device_id=(to_dp, to_vocab),
                device_id_type=MESH,
            ),
            pltpu.make_async_remote_copy(
                src_ref=part(to_dp, to_vocab),
                dst_ref=arr_ref.at[slot],
                send_sem=send_sem.at[k],
                recv_sem=arrive_sem.at[slot],
                device_id=(to_dp, to_vocab),
                device_id_type=MESH,
            ),
        )

    def send_pair(k):
        to_dp = lax.rem(k // owners + 1, groups)
        to_vocab = lax.rem(my_vocab + lax.rem(k, owners), owners)
        here = (to_dp == my_dp) & (to_vocab == my_vocab)
        return here, pair(k, me, to_dp, to_vocab)

    def send(k, carry):
        here, copies = send_pair(k)

        @pl.when(jnp.logical_not(here))
        def _():
            copies[0].start()
            copies[1].start()

        return carry

    lax.fori_loop(0, total, send, 0)

    def arrive(k, carry):
        sender = lax.rem(me + k, total)
        tag, grads = pair(k, sender, sender // owners, lax.rem(sender, owners))
        tag.wait_recv()
        grads.wait_recv()
        return carry

    for load in loads:
        load.wait()
    own.wait()
    own_tag.wait()
    lax.fori_loop(1, total, arrive, 0)

    tokens = total * CAP
    pairs = tag_ref[...].astype(jnp.float32).reshape(tokens, LANES)
    decoded = jnp.broadcast_to(pairs[:, 0:1] * 16.0 + pairs[:, 1:2], (tokens, LANES)).T[0:1, :]
    grads = arr_ref[...].astype(jnp.float32).reshape(tokens, columns).astype(jnp.bfloat16)

    def place(block, chunk):
        start = pl.multiple_of(block * columns, LANES)
        return table_ref.at[pl.ds(chunk * step_rows, step_rows), pl.ds(start, columns)]

    def copy(block, chunk, step, sem, to_dp):
        source = (
            block_ref.at[pl.ds(chunk * step_rows, step_rows), :] if step == 0 else place(block, chunk)
        )
        return pltpu.make_async_remote_copy(
            src_ref=source,
            dst_ref=place(block, chunk),
            send_sem=sem.at[step, chunk],
            recv_sem=recv_sem.at[block, chunk],
            device_id={"dp": to_dp},
            device_id_type=MESH,
        )

    def both(act, step, chunk):
        upper, lower = my_dp + step, my_dp - step
        pl.when(upper < groups)(functools.partial(act, upper, chunk, step, left_sem, my_dp - 1, has_left))
        pl.when(lower >= 0)(functools.partial(act, lower, chunk, step, right_sem, my_dp + 1, has_right))

    def held_back(step, chunk):
        return step >= groups - 1 and chunk >= kept

    def start(block, chunk, step, sem, to_dp, sends):
        if step > 0:
            copy(block, chunk, step, sem, my_dp).wait_recv()
        if not held_back(step + 1, chunk):

            @pl.when(sends)
            def _():
                copy(block, chunk, step, sem, to_dp).start()

    def drain(block, chunk, step, sem, to_dp, sends):
        if not held_back(step + 1, chunk):

            @pl.when(sends)
            def _():
                copy(block, chunk, step, sem, to_dp).wait_send()

    row_iota = lax.broadcasted_iota(jnp.int32, (step_rows, tokens), 0)
    for chunk in range(CHUNKS):
        here = pl.ds(chunk * step_rows, step_rows)
        selector = decoded == (row_iota + chunk * step_rows).astype(jnp.float32)
        gradient = jnp.dot(
            selector.astype(jnp.float32).astype(jnp.bfloat16), grads, preferred_element_type=jnp.float32
        )
        master, first, second = adam(gradient, master_ref[here, :], first_ref[here, :], second_ref[here, :])
        block_ref[here, :] = master.astype(jnp.bfloat16)
        master_ref[here, :] = master
        first_ref[here, :] = first
        second_ref[here, :] = second
        if chunk > 0:
            both(start, 0, chunk - 1)
    both(start, 0, CHUNKS - 1)
    own_block = pltpu.make_async_copy(
        block_ref,
        table_ref.at[:, pl.ds(pl.multiple_of(my_dp * columns, LANES), columns)],
        own_sem.at[1],
    )
    own_block.start()
    for step in range(1, groups):
        for chunk in range(CHUNKS):
            if not held_back(step, chunk):
                both(start, step, chunk)
    for step in range(groups):
        for chunk in range(CHUNKS):
            if not held_back(step, chunk):
                both(drain, step, chunk)

    def sent(k, carry):
        here, copies = send_pair(k)

        @pl.when(jnp.logical_not(here))
        def _():
            copies[0].wait_send()
            copies[1].wait_send()

        return carry

    lax.fori_loop(0, total, sent, 0)
    own_block.wait()


def exchange_and_gather(outgoing, ids, master, first, second, groups, kept):
    owners = ids.shape[0]
    total = groups * owners
    rows, columns = master.shape
    anywhere = pl.BlockSpec(memory_space=pl.ANY)
    held = pl.BlockSpec(memory_space=pltpu.VMEM)
    return pl.pallas_call(
        functools.partial(step_kernel, groups, owners, kept),
        out_shape=(
            pltpu.VMEM((rows, columns * groups), jnp.bfloat16),
            pltpu.VMEM((rows, columns), jnp.float32),
            pltpu.VMEM((rows, columns), jnp.float32),
            pltpu.VMEM((rows, columns), jnp.float32),
        ),
        in_specs=[anywhere] * 2 + [pl.BlockSpec(memory_space=pltpu.HBM)] * 3,
        out_specs=(held, held, held, held),
        scratch_shapes=[
            pltpu.VMEM((total, CAP, columns), jnp.bfloat16),
            pltpu.VMEM((total, CAP, LANES), jnp.bfloat16),
            pltpu.VMEM((rows, columns), jnp.bfloat16),
            pltpu.SemaphoreType.DMA((total,)),
            pltpu.SemaphoreType.DMA((total,)),
            pltpu.SemaphoreType.DMA((total,)),
            pltpu.SemaphoreType.DMA((total,)),
            pltpu.SemaphoreType.DMA((groups, CHUNKS)),
            pltpu.SemaphoreType.DMA((groups, CHUNKS)),
            pltpu.SemaphoreType.DMA((groups, CHUNKS)),
            pltpu.SemaphoreType.DMA((3,)),
            pltpu.SemaphoreType.DMA((3,)),
        ],
        compiler_params=pltpu.CompilerParams(
            collective_id=0, has_side_effects=True, vmem_limit_bytes=20 * 2**20
        ),
        name="exchange_and_gather",
    )(outgoing, ids, master, first, second)


def copy_kernel(src_ref, dst_ref):
    dst_ref[...] = src_ref[...]


def fresh_copy(table):
    rows, width = table.shape
    block = pl.BlockSpec((rows // CHUNKS, width), lambda i: (i, 0))
    return pl.pallas_call(
        copy_kernel,
        out_shape=jax.ShapeDtypeStruct(table.shape, table.dtype),
        grid=(CHUNKS,),
        in_specs=[block],
        out_specs=block,
        cost_estimate=pl.CostEstimate(flops=0, bytes_accessed=4 * rows * width, transcendentals=0),
        name="fresh_copy",
    )(table)


def patch_kernel(groups, tail_ref, old_ref, table_ref, sem):
    my_dp = lax.axis_index("dp")
    rows, columns = tail_ref.shape
    top = table_ref.shape[0] - rows
    far = pl.multiple_of(jnp.where(my_dp == 0, groups - 1, 0) * columns, LANES)

    @pl.when((my_dp == 0) | (my_dp == groups - 1))
    def _():
        copy = pltpu.make_async_copy(tail_ref, table_ref.at[pl.ds(top, rows), pl.ds(far, columns)], sem)
        copy.start()
        copy.wait()


def patch(tail, table, groups):
    return pl.pallas_call(
        functools.partial(patch_kernel, groups),
        out_shape=jax.ShapeDtypeStruct(table.shape, table.dtype),
        in_specs=[pl.BlockSpec(memory_space=pltpu.VMEM), pl.BlockSpec(memory_space=pl.ANY)],
        out_specs=pl.BlockSpec(memory_space=pl.ANY),
        scratch_shapes=[pltpu.SemaphoreType.DMA],
        input_output_aliases={1: 0},
        name="patch",
    )(tail, table)


def body(token_ids, token_count, out_grads, master_rows, first_moment, second_moment):
    owners = lax.axis_size("vocab")
    groups = lax.axis_size("dp")
    rows_own, columns = master_rows.shape
    tok_slots = token_ids.shape[0]
    first_new = VOCAB - rows_own * owners
    position = jnp.arange(tok_slots)
    is_live = (position < token_count[0]) & (token_ids >= first_new)
    new_index = token_ids - first_new
    owner_of = jnp.where(is_live, new_index // rows_own, -1)
    row_in_owner = new_index % rows_own
    earlier = (owner_of[:, None] == owner_of[None, :]) & (position[:, None] < position[None, :])
    my_rank = jnp.sum(earlier.astype(jnp.int32), axis=0)
    slot_index = jnp.where(is_live, owner_of * CAP + my_rank, -1)
    placing = jnp.arange(owners * CAP)[:, None] == slot_index[None, :]
    outgoing = jnp.dot(
        placing.astype(jnp.bfloat16), out_grads, preferred_element_type=jnp.float32
    ).astype(jnp.bfloat16)
    slot_row = jnp.max(jnp.where(placing, row_in_owner[None, :], -1), axis=1)
    upper_part = jnp.where(slot_row >= 0, slot_row // 16, -1)
    lower_part = jnp.where(slot_row >= 0, slot_row % 16, 0)
    lane = jnp.arange(LANES)[None, :]
    row_pairs = jnp.where(lane == 0, upper_part[:, None], jnp.where(lane == 1, lower_part[:, None], 0))
    row_pairs = row_pairs.astype(jnp.bfloat16).reshape(owners, CAP, LANES)
    kept = KEPT if groups >= 4 else CHUNKS
    table, new_master, new_first, new_second = exchange_and_gather(
        outgoing, row_pairs, master_rows, first_moment, second_moment, groups, kept
    )
    if kept < CHUNKS:
        my_dp = lax.axis_index("dp")
        top = rows_own // CHUNKS * kept
        sent = jnp.where(my_dp == 1, groups - 1, 0) * columns
        tail = lax.dynamic_slice(table, (top, sent), (rows_own - top, columns))
        tail = lax.ppermute(tail, "dp", [(1, 0), (groups - 2, groups - 1)])
        table = patch(tail, fresh_copy(table), groups)
    return (new_master, new_first, new_second, table)


def solution(mesh):
    return jax.shard_map(
        body,
        mesh=mesh,
        in_specs=(
            P(("dp", "vocab")),
            P(("dp", "vocab")),
            P(("dp", "vocab"), None),
            P("vocab", "dp"),
            P("vocab", "dp"),
            P("vocab", "dp"),
        ),
        out_specs=(P("vocab", "dp"), P("vocab", "dp"), P("vocab", "dp"), P("vocab", None)),
        check_vma=False,
    )
```

```python
import functools

import jax
import jax.numpy as jnp
from jax import lax
from jax.experimental import pallas as pl
from jax.experimental.pallas import tpu as pltpu
from jax.sharding import PartitionSpec as P

VOCAB = 152064
CAP = 8
LANES = 128
CHUNKS = 8
KEPT = 8
MESH = pl.DeviceIdType.MESH


beta_one = 0.9
beta_two = 0.999
corr_one = 1.0 - 0.9**10
corr_two = 1.0 - 0.999**10
learn_rate = 0.01
epsilon = 1e-08


def adam(gradient, master, first, second):
    new_first = beta_one * first + (1.0 - beta_one) * gradient
    new_second = beta_two * second + (1.0 - beta_two) * gradient * gradient
    update = new_first / corr_one / (jnp.sqrt(new_second / corr_two) + epsilon)
    return master - learn_rate * update, new_first, new_second


def step_kernel(
    groups,
    owners,
    kept,
    out_ref,
    ids_ref,
    master_hbm,
    first_hbm,
    second_hbm,
    table_ref,
    master_ref,
    first_ref,
    second_ref,
    arr_ref,
    tag_ref,
    block_ref,
    send_sem,
    arrive_sem,
    tag_send_sem,
    tag_sem,
    left_sem,
    right_sem,
    recv_sem,
    own_sem,
    load_sem,
):
    my_dp, my_vocab = lax.axis_index("dp"), lax.axis_index("vocab")
    total = groups * owners
    me = my_dp * owners + my_vocab
    rows, columns = master_ref.shape
    step_rows = rows // CHUNKS
    barrier = pltpu.get_barrier_semaphore()
    has_left, has_right = my_dp > 0, my_dp < groups - 1

    loads = [
        pltpu.make_async_copy(src, dst, load_sem.at[i])
        for i, (src, dst) in enumerate(
            ((master_hbm, master_ref), (first_hbm, first_ref), (second_hbm, second_ref))
        )
    ]
    for load in loads:
        load.start()

    def greet(k, carry):
        other = lax.rem(me + k, total)
        pl.semaphore_signal(
            barrier, inc=1, device_id=(other // owners, lax.rem(other, owners)), device_id_type=MESH
        )
        return carry

    lax.fori_loop(1, total, greet, 0)
    def part(to_dp, to_vocab):
        row = pl.multiple_of(to_vocab * CAP, CAP)
        return out_ref.at[pl.ds(row, CAP), pl.ds(pl.multiple_of(to_dp * columns, LANES), columns)]

    own = pltpu.make_async_copy(part(my_dp, my_vocab), arr_ref.at[me], own_sem.at[0])
    own.start()
    own_tag = pltpu.make_async_copy(ids_ref.at[my_vocab], tag_ref.at[me], own_sem.at[2])
    own_tag.start()
    pl.semaphore_wait(barrier, total - 1)

    def pair(k, slot, to_dp, to_vocab):
        return (
            pltpu.make_async_remote_copy(
                src_ref=ids_ref.at[to_vocab],
                dst_ref=tag_ref.at[slot],
                send_sem=tag_send_sem.at[k],
                recv_sem=tag_sem.at[slot],
                device_id=(to_dp, to_vocab),
                device_id_type=MESH,
            ),
            pltpu.make_async_remote_copy(
                src_ref=part(to_dp, to_vocab),
                dst_ref=arr_ref.at[slot],
                send_sem=send_sem.at[k],
                recv_sem=arrive_sem.at[slot],
                device_id=(to_dp, to_vocab),
                device_id_type=MESH,
            ),
        )

    def send_pair(k):
        to_dp = lax.rem(k // owners + 1, groups)
        to_vocab = lax.rem(my_vocab + lax.rem(k, owners), owners)
        here = (to_dp == my_dp) & (to_vocab == my_vocab)
        return here, pair(k, me, to_dp, to_vocab)

    def send(k, carry):
        here, copies = send_pair(k)

        @pl.when(jnp.logical_not(here))
        def _():
            copies[0].start()
            copies[1].start()

        return carry

    lax.fori_loop(0, total, send, 0)

    def arrive(k, carry):
        sender = lax.rem(me + k, total)
        tag, grads = pair(k, sender, sender // owners, lax.rem(sender, owners))
        tag.wait_recv()
        grads.wait_recv()
        return carry

    for load in loads:
        load.wait()
    own.wait()
    own_tag.wait()
    lax.fori_loop(1, total, arrive, 0)

    tokens = total * CAP
    pairs = tag_ref[...].astype(jnp.float32).reshape(tokens, LANES)
    decoded = jnp.broadcast_to(pairs[:, 0:1] * 16.0 + pairs[:, 1:2], (tokens, LANES)).T[0:1, :]
    grads = arr_ref[...].astype(jnp.float32).reshape(tokens, columns).astype(jnp.bfloat16)

    def place(block, chunk):
        start = pl.multiple_of(block * columns, LANES)
        return table_ref.at[pl.ds(chunk * step_rows, step_rows), pl.ds(start, columns)]

    def copy(block, chunk, step, sem, to_dp):
        source = (
            block_ref.at[pl.ds(chunk * step_rows, step_rows), :] if step == 0 else place(block, chunk)
        )
        return pltpu.make_async_remote_copy(
            src_ref=source,
            dst_ref=place(block, chunk),
            send_sem=sem.at[step, chunk],
            recv_sem=recv_sem.at[block, chunk],
            device_id={"dp": to_dp},
            device_id_type=MESH,
        )

    def both(act, step, chunk):
        upper, lower = my_dp + step, my_dp - step
        pl.when(upper < groups)(functools.partial(act, upper, chunk, step, left_sem, my_dp - 1, has_left))
        pl.when(lower >= 0)(functools.partial(act, lower, chunk, step, right_sem, my_dp + 1, has_right))

    def held_back(step, chunk):
        return step >= groups - 1 and chunk >= kept

    def start(block, chunk, step, sem, to_dp, sends):
        if step > 0:
            copy(block, chunk, step, sem, my_dp).wait_recv()
        if not held_back(step + 1, chunk):

            @pl.when(sends)
            def _():
                copy(block, chunk, step, sem, to_dp).start()

    def drain(block, chunk, step, sem, to_dp, sends):
        if not held_back(step + 1, chunk):

            @pl.when(sends)
            def _():
                copy(block, chunk, step, sem, to_dp).wait_send()

    row_iota = lax.broadcasted_iota(jnp.int32, (step_rows, tokens), 0)
    for chunk in range(CHUNKS):
        here = pl.ds(chunk * step_rows, step_rows)
        selector = decoded == (row_iota + chunk * step_rows).astype(jnp.float32)
        gradient = jnp.dot(
            selector.astype(jnp.float32).astype(jnp.bfloat16), grads, preferred_element_type=jnp.float32
        )
        master, first, second = adam(gradient, master_ref[here, :], first_ref[here, :], second_ref[here, :])
        block_ref[here, :] = master.astype(jnp.bfloat16)
        master_ref[here, :] = master
        first_ref[here, :] = first
        second_ref[here, :] = second
        if chunk > 0:
            both(start, 0, chunk - 1)
    both(start, 0, CHUNKS - 1)
    own_block = pltpu.make_async_copy(
        block_ref,
        table_ref.at[:, pl.ds(pl.multiple_of(my_dp * columns, LANES), columns)],
        own_sem.at[1],
    )
    own_block.start()
    for step in range(1, groups):
        for chunk in range(CHUNKS):
            if not held_back(step, chunk):
                both(start, step, chunk)
    for step in range(groups):
        for chunk in range(CHUNKS):
            if not held_back(step, chunk):
                both(drain, step, chunk)

    def sent(k, carry):
        here, copies = send_pair(k)

        @pl.when(jnp.logical_not(here))
        def _():
            copies[0].wait_send()
            copies[1].wait_send()

        return carry

    lax.fori_loop(0, total, sent, 0)
    own_block.wait()


def exchange_and_gather(outgoing, ids, master, first, second, groups, kept):
    owners = ids.shape[0]
    total = groups * owners
    rows, columns = master.shape
    anywhere = pl.BlockSpec(memory_space=pl.ANY)
    held = pl.BlockSpec(memory_space=pltpu.VMEM)
    return pl.pallas_call(
        functools.partial(step_kernel, groups, owners, kept),
        out_shape=(
            pltpu.VMEM((rows, columns * groups), jnp.bfloat16),
            pltpu.VMEM((rows, columns), jnp.float32),
            pltpu.VMEM((rows, columns), jnp.float32),
            pltpu.VMEM((rows, columns), jnp.float32),
        ),
        in_specs=[anywhere] * 2 + [pl.BlockSpec(memory_space=pltpu.HBM)] * 3,
        out_specs=(held, held, held, held),
        scratch_shapes=[
            pltpu.VMEM((total, CAP, columns), jnp.bfloat16),
            pltpu.VMEM((total, CAP, LANES), jnp.bfloat16),
            pltpu.VMEM((rows, columns), jnp.bfloat16),
            pltpu.SemaphoreType.DMA((total,)),
            pltpu.SemaphoreType.DMA((total,)),
            pltpu.SemaphoreType.DMA((total,)),
            pltpu.SemaphoreType.DMA((total,)),
            pltpu.SemaphoreType.DMA((groups, CHUNKS)),
            pltpu.SemaphoreType.DMA((groups, CHUNKS)),
            pltpu.SemaphoreType.DMA((groups, CHUNKS)),
            pltpu.SemaphoreType.DMA((3,)),
            pltpu.SemaphoreType.DMA((3,)),
        ],
        compiler_params=pltpu.CompilerParams(
            collective_id=0, has_side_effects=True, vmem_limit_bytes=20 * 2**20
        ),
        name="exchange_and_gather",
    )(outgoing, ids, *(pltpu.with_memory_space_constraint(x, pltpu.HBM) for x in (master, first, second)))


def copy_kernel(src_ref, dst_ref):
    dst_ref[...] = src_ref[...]


def fresh_copy(table):
    rows, width = table.shape
    block = pl.BlockSpec((rows // CHUNKS, width), lambda i: (i, 0))
    return pl.pallas_call(
        copy_kernel,
        out_shape=jax.ShapeDtypeStruct(table.shape, table.dtype),
        grid=(CHUNKS,),
        in_specs=[block],
        out_specs=block,
        cost_estimate=pl.CostEstimate(flops=0, bytes_accessed=4 * rows * width, transcendentals=0),
        name="fresh_copy",
    )(table)


def patch_kernel(groups, tail_ref, old_ref, table_ref, sem):
    my_dp = lax.axis_index("dp")
    rows, columns = tail_ref.shape
    top = table_ref.shape[0] - rows
    far = pl.multiple_of(jnp.where(my_dp == 0, groups - 1, 0) * columns, LANES)

    @pl.when((my_dp == 0) | (my_dp == groups - 1))
    def _():
        copy = pltpu.make_async_copy(tail_ref, table_ref.at[pl.ds(top, rows), pl.ds(far, columns)], sem)
        copy.start()
        copy.wait()


def patch(tail, table, groups):
    return pl.pallas_call(
        functools.partial(patch_kernel, groups),
        out_shape=jax.ShapeDtypeStruct(table.shape, table.dtype),
        in_specs=[pl.BlockSpec(memory_space=pltpu.VMEM), pl.BlockSpec(memory_space=pl.ANY)],
        out_specs=pl.BlockSpec(memory_space=pl.ANY),
        scratch_shapes=[pltpu.SemaphoreType.DMA],
        input_output_aliases={1: 0},
        name="patch",
    )(tail, table)


def body(token_ids, token_count, out_grads, master_rows, first_moment, second_moment):
    owners = lax.axis_size("vocab")
    groups = lax.axis_size("dp")
    rows_own, columns = master_rows.shape
    tok_slots = token_ids.shape[0]
    first_new = VOCAB - rows_own * owners
    position = jnp.arange(tok_slots)
    is_live = (position < token_count[0]) & (token_ids >= first_new)
    new_index = token_ids - first_new
    owner_of = jnp.where(is_live, new_index // rows_own, -1)
    row_in_owner = new_index % rows_own
    earlier = (owner_of[:, None] == owner_of[None, :]) & (position[:, None] < position[None, :])
    my_rank = jnp.sum(earlier.astype(jnp.int32), axis=0)
    slot_index = jnp.where(is_live, owner_of * CAP + my_rank, -1)
    placing = jnp.arange(owners * CAP)[:, None] == slot_index[None, :]
    outgoing = jnp.dot(
        placing.astype(jnp.bfloat16), out_grads, preferred_element_type=jnp.float32
    ).astype(jnp.bfloat16)
    slot_row = jnp.max(jnp.where(placing, row_in_owner[None, :], -1), axis=1)
    upper_part = jnp.where(slot_row >= 0, slot_row // 16, -1)
    lower_part = jnp.where(slot_row >= 0, slot_row % 16, 0)
    lane = jnp.arange(LANES)[None, :]
    row_pairs = jnp.where(lane == 0, upper_part[:, None], jnp.where(lane == 1, lower_part[:, None], 0))
    row_pairs = row_pairs.astype(jnp.bfloat16).reshape(owners, CAP, LANES)
    kept = KEPT if groups >= 4 else CHUNKS
    table, new_master, new_first, new_second = exchange_and_gather(
        outgoing, row_pairs, master_rows, first_moment, second_moment, groups, kept
    )
    if kept < CHUNKS:
        my_dp = lax.axis_index("dp")
        top = rows_own // CHUNKS * kept
        sent = jnp.where(my_dp == 1, groups - 1, 0) * columns
        tail = lax.dynamic_slice(table, (top, sent), (rows_own - top, columns))
        tail = lax.ppermute(tail, "dp", [(1, 0), (groups - 2, groups - 1)])
        table = patch(tail, fresh_copy(table), groups)
    return (new_master, new_first, new_second, table)


def solution(mesh):
    return jax.shard_map(
        body,
        mesh=mesh,
        in_specs=(
            P(("dp", "vocab")),
            P(("dp", "vocab")),
            P(("dp", "vocab"), None),
            P("vocab", "dp"),
            P("vocab", "dp"),
            P("vocab", "dp"),
        ),
        out_specs=(P("vocab", "dp"), P("vocab", "dp"), P("vocab", "dp"), P("vocab", None)),
        check_vma=False,
    )
```

```python
import functools

import jax
import jax.numpy as jnp
from jax import lax
from jax.experimental import pallas as pl
from jax.experimental.pallas import tpu as pltpu
from jax.sharding import PartitionSpec as P

VOCAB = 152064
CAP = 8
LANES = 128
CHUNKS = 8
KEPT = 6
MESH = pl.DeviceIdType.MESH


beta_one = 0.9
beta_two = 0.999
corr_one = 1.0 - 0.9**10
corr_two = 1.0 - 0.999**10
learn_rate = 0.01
epsilon = 1e-08


def adam(gradient, master, first, second):
    new_first = beta_one * first + (1.0 - beta_one) * gradient
    new_second = beta_two * second + (1.0 - beta_two) * gradient * gradient
    update = new_first / corr_one / (jnp.sqrt(new_second / corr_two) + epsilon)
    return master - learn_rate * update, new_first, new_second


def step_kernel(
    groups,
    owners,
    kept,
    out_ref,
    ids_ref,
    master_hbm,
    first_hbm,
    second_hbm,
    table_ref,
    master_ref,
    first_ref,
    second_ref,
    arr_ref,
    tag_ref,
    block_ref,
    send_sem,
    arrive_sem,
    tag_send_sem,
    tag_sem,
    left_sem,
    right_sem,
    recv_sem,
    own_sem,
    load_sem,
):
    my_dp, my_vocab = lax.axis_index("dp"), lax.axis_index("vocab")
    total = groups * owners
    me = my_dp * owners + my_vocab
    rows, columns = master_ref.shape
    step_rows = rows // CHUNKS
    barrier = pltpu.get_barrier_semaphore()
    has_left, has_right = my_dp > 0, my_dp < groups - 1

    loads = [
        pltpu.make_async_copy(src, dst, load_sem.at[i])
        for i, (src, dst) in enumerate(
            ((master_hbm, master_ref), (first_hbm, first_ref), (second_hbm, second_ref))
        )
    ]
    for load in loads:
        load.start()

    def greet(k, carry):
        other = lax.rem(me + k, total)
        pl.semaphore_signal(
            barrier, inc=1, device_id=(other // owners, lax.rem(other, owners)), device_id_type=MESH
        )
        return carry

    lax.fori_loop(1, total, greet, 0)
    def part(to_dp, to_vocab):
        row = pl.multiple_of(to_vocab * CAP, CAP)
        return out_ref.at[pl.ds(row, CAP), pl.ds(pl.multiple_of(to_dp * columns, LANES), columns)]

    own = pltpu.make_async_copy(part(my_dp, my_vocab), arr_ref.at[me], own_sem.at[0])
    own.start()
    own_tag = pltpu.make_async_copy(ids_ref.at[my_vocab], tag_ref.at[me], own_sem.at[2])
    own_tag.start()
    pl.semaphore_wait(barrier, total - 1)

    def pair(k, slot, to_dp, to_vocab):
        return (
            pltpu.make_async_remote_copy(
                src_ref=ids_ref.at[to_vocab],
                dst_ref=tag_ref.at[slot],
                send_sem=tag_send_sem.at[k],
                recv_sem=tag_sem.at[slot],
                device_id=(to_dp, to_vocab),
                device_id_type=MESH,
            ),
            pltpu.make_async_remote_copy(
                src_ref=part(to_dp, to_vocab),
                dst_ref=arr_ref.at[slot],
                send_sem=send_sem.at[k],
                recv_sem=arrive_sem.at[slot],
                device_id=(to_dp, to_vocab),
                device_id_type=MESH,
            ),
        )

    def send_pair(k):
        to_dp = lax.rem(k // owners + 1, groups)
        to_vocab = lax.rem(my_vocab + lax.rem(k, owners), owners)
        here = (to_dp == my_dp) & (to_vocab == my_vocab)
        return here, pair(k, me, to_dp, to_vocab)

    def send(k, carry):
        here, copies = send_pair(k)

        @pl.when(jnp.logical_not(here))
        def _():
            copies[0].start()
            copies[1].start()

        return carry

    lax.fori_loop(0, total, send, 0)

    def arrive(k, carry):
        sender = lax.rem(me + k, total)
        tag, grads = pair(k, sender, sender // owners, lax.rem(sender, owners))
        tag.wait_recv()
        grads.wait_recv()
        return carry

    for load in loads:
        load.wait()
    own.wait()
    own_tag.wait()
    lax.fori_loop(1, total, arrive, 0)

    tokens = total * CAP
    pairs = tag_ref[...].astype(jnp.float32).reshape(tokens, LANES)
    decoded = jnp.broadcast_to(pairs[:, 0:1] * 16.0 + pairs[:, 1:2], (tokens, LANES)).T[0:1, :]
    grads = arr_ref[...].astype(jnp.float32).reshape(tokens, columns).astype(jnp.bfloat16)

    def place(block, chunk):
        start = pl.multiple_of(block * columns, LANES)
        return table_ref.at[pl.ds(chunk * step_rows, step_rows), pl.ds(start, columns)]

    def copy(block, chunk, step, sem, to_dp):
        source = (
            block_ref.at[pl.ds(chunk * step_rows, step_rows), :] if step == 0 else place(block, chunk)
        )
        return pltpu.make_async_remote_copy(
            src_ref=source,
            dst_ref=place(block, chunk),
            send_sem=sem.at[step, chunk],
            recv_sem=recv_sem.at[block, chunk],
            device_id={"dp": to_dp},
            device_id_type=MESH,
        )

    def both(act, step, chunk):
        upper, lower = my_dp + step, my_dp - step
        pl.when(upper < groups)(functools.partial(act, upper, chunk, step, left_sem, my_dp - 1, has_left))
        pl.when(lower >= 0)(functools.partial(act, lower, chunk, step, right_sem, my_dp + 1, has_right))

    def held_back(step, chunk):
        return step >= groups - 1 and chunk >= kept

    def start(block, chunk, step, sem, to_dp, sends):
        if step > 0:
            copy(block, chunk, step, sem, my_dp).wait_recv()
        if not held_back(step + 1, chunk):

            @pl.when(sends)
            def _():
                copy(block, chunk, step, sem, to_dp).start()

    def drain(block, chunk, step, sem, to_dp, sends):
        if not held_back(step + 1, chunk):

            @pl.when(sends)
            def _():
                copy(block, chunk, step, sem, to_dp).wait_send()

    row_iota = lax.broadcasted_iota(jnp.int32, (step_rows, tokens), 0)
    for chunk in range(CHUNKS):
        here = pl.ds(chunk * step_rows, step_rows)
        selector = decoded == (row_iota + chunk * step_rows).astype(jnp.float32)
        gradient = jnp.dot(
            selector.astype(jnp.float32).astype(jnp.bfloat16), grads, preferred_element_type=jnp.float32
        )
        master, first, second = adam(gradient, master_ref[here, :], first_ref[here, :], second_ref[here, :])
        block_ref[here, :] = master.astype(jnp.bfloat16)
        master_ref[here, :] = master
        first_ref[here, :] = first
        second_ref[here, :] = second
        if chunk > 0:
            both(start, 0, chunk - 1)
    both(start, 0, CHUNKS - 1)
    own_block = pltpu.make_async_copy(
        block_ref,
        table_ref.at[:, pl.ds(pl.multiple_of(my_dp * columns, LANES), columns)],
        own_sem.at[1],
    )
    own_block.start()
    for step in range(1, groups):
        for chunk in range(CHUNKS):
            if not held_back(step, chunk):
                both(start, step, chunk)
    for step in range(groups):
        for chunk in range(CHUNKS):
            if not held_back(step, chunk):
                both(drain, step, chunk)

    def sent(k, carry):
        here, copies = send_pair(k)

        @pl.when(jnp.logical_not(here))
        def _():
            copies[0].wait_send()
            copies[1].wait_send()

        return carry

    lax.fori_loop(0, total, sent, 0)
    own_block.wait()


def exchange_and_gather(outgoing, ids, master, first, second, groups, kept):
    owners = ids.shape[0]
    total = groups * owners
    rows, columns = master.shape
    anywhere = pl.BlockSpec(memory_space=pl.ANY)
    held = pl.BlockSpec(memory_space=pltpu.VMEM)
    return pl.pallas_call(
        functools.partial(step_kernel, groups, owners, kept),
        out_shape=(
            pltpu.VMEM((rows, columns * groups), jnp.bfloat16),
            pltpu.VMEM((rows, columns), jnp.float32),
            pltpu.VMEM((rows, columns), jnp.float32),
            pltpu.VMEM((rows, columns), jnp.float32),
        ),
        in_specs=[anywhere] * 2 + [pl.BlockSpec(memory_space=pltpu.HBM)] * 3,
        out_specs=(held, held, held, held),
        scratch_shapes=[
            pltpu.VMEM((total, CAP, columns), jnp.bfloat16),
            pltpu.VMEM((total, CAP, LANES), jnp.bfloat16),
            pltpu.VMEM((rows, columns), jnp.bfloat16),
            pltpu.SemaphoreType.DMA((total,)),
            pltpu.SemaphoreType.DMA((total,)),
            pltpu.SemaphoreType.DMA((total,)),
            pltpu.SemaphoreType.DMA((total,)),
            pltpu.SemaphoreType.DMA((groups, CHUNKS)),
            pltpu.SemaphoreType.DMA((groups, CHUNKS)),
            pltpu.SemaphoreType.DMA((groups, CHUNKS)),
            pltpu.SemaphoreType.DMA((3,)),
            pltpu.SemaphoreType.DMA((3,)),
        ],
        compiler_params=pltpu.CompilerParams(
            collective_id=0, has_side_effects=True, vmem_limit_bytes=20 * 2**20
        ),
        name="exchange_and_gather",
    )(outgoing, ids, *(pltpu.with_memory_space_constraint(x, pltpu.HBM) for x in (master, first, second)))


def copy_kernel(src_ref, dst_ref, sem):
    copy = pltpu.make_async_copy(src_ref, dst_ref, sem)
    copy.start()
    copy.wait()


def fresh_copy(table):
    rows, width = table.shape
    anywhere = pl.BlockSpec(memory_space=pl.ANY)
    return pl.pallas_call(
        copy_kernel,
        out_shape=pltpu.HBM(table.shape, table.dtype),
        in_specs=[anywhere],
        out_specs=anywhere,
        scratch_shapes=[pltpu.SemaphoreType.DMA],
        cost_estimate=pl.CostEstimate(flops=0, bytes_accessed=4 * rows * width, transcendentals=0),
        compiler_params=pltpu.CompilerParams(vmem_limit_bytes=2**20),
        name="fresh_copy",
    )(table)


def patch_kernel(groups, tail_ref, old_ref, table_ref, sem):
    my_dp = lax.axis_index("dp")
    rows, columns = tail_ref.shape
    top = table_ref.shape[0] - rows
    far = pl.multiple_of(jnp.where(my_dp == 0, groups - 1, 0) * columns, LANES)

    @pl.when((my_dp == 0) | (my_dp == groups - 1))
    def _():
        copy = pltpu.make_async_copy(tail_ref, table_ref.at[pl.ds(top, rows), pl.ds(far, columns)], sem)
        copy.start()
        copy.wait()


def patch(tail, table, groups):
    return pl.pallas_call(
        functools.partial(patch_kernel, groups),
        out_shape=jax.ShapeDtypeStruct(table.shape, table.dtype),
        in_specs=[pl.BlockSpec(memory_space=pl.ANY), pl.BlockSpec(memory_space=pl.ANY)],
        out_specs=pl.BlockSpec(memory_space=pl.ANY),
        scratch_shapes=[pltpu.SemaphoreType.DMA],
        input_output_aliases={1: 0},
        compiler_params=pltpu.CompilerParams(vmem_limit_bytes=2**20),
        name="patch",
    )(tail, table)


def body(token_ids, token_count, out_grads, master_rows, first_moment, second_moment):
    owners = lax.axis_size("vocab")
    groups = lax.axis_size("dp")
    rows_own, columns = master_rows.shape
    tok_slots = token_ids.shape[0]
    first_new = VOCAB - rows_own * owners
    position = jnp.arange(tok_slots)
    is_live = (position < token_count[0]) & (token_ids >= first_new)
    new_index = token_ids - first_new
    owner_of = jnp.where(is_live, new_index // rows_own, -1)
    row_in_owner = new_index % rows_own
    earlier = (owner_of[:, None] == owner_of[None, :]) & (position[:, None] < position[None, :])
    my_rank = jnp.sum(earlier.astype(jnp.int32), axis=0)
    slot_index = jnp.where(is_live, owner_of * CAP + my_rank, -1)
    placing = jnp.arange(owners * CAP)[:, None] == slot_index[None, :]
    outgoing = jnp.dot(
        placing.astype(jnp.bfloat16), out_grads, preferred_element_type=jnp.float32
    ).astype(jnp.bfloat16)
    slot_row = jnp.max(jnp.where(placing, row_in_owner[None, :], -1), axis=1)
    upper_part = jnp.where(slot_row >= 0, slot_row // 16, -1)
    lower_part = jnp.where(slot_row >= 0, slot_row % 16, 0)
    lane = jnp.arange(LANES)[None, :]
    row_pairs = jnp.where(lane == 0, upper_part[:, None], jnp.where(lane == 1, lower_part[:, None], 0))
    row_pairs = row_pairs.astype(jnp.bfloat16).reshape(owners, CAP, LANES)
    kept = KEPT if groups >= 4 else CHUNKS
    table, new_master, new_first, new_second = exchange_and_gather(
        outgoing, row_pairs, master_rows, first_moment, second_moment, groups, kept
    )
    if kept < CHUNKS:
        my_dp = lax.axis_index("dp")
        top = rows_own // CHUNKS * kept
        sent = jnp.where(my_dp == 1, groups - 1, 0) * columns
        tail = lax.dynamic_slice(table, (top, sent), (rows_own - top, columns))
        tail = lax.ppermute(tail, "dp", [(1, 0), (groups - 2, groups - 1)])
        table = patch(tail, fresh_copy(table), groups)
    return (new_master, new_first, new_second, table)


def solution(mesh):
    return jax.shard_map(
        body,
        mesh=mesh,
        in_specs=(
            P(("dp", "vocab")),
            P(("dp", "vocab")),
            P(("dp", "vocab"), None),
            P("vocab", "dp"),
            P("vocab", "dp"),
            P("vocab", "dp"),
        ),
        out_specs=(P("vocab", "dp"), P("vocab", "dp"), P("vocab", "dp"), P("vocab", None)),
        check_vma=False,
    )
```
